32 devices in a mesh: inst: 4 (over z), sector: 4 (over y, core), slab: 2 (over x).
Axes of the slice: x: 2, y: 2, z: 4, core: 2. Of those that a mesh axis runs over, the one named last changes fastest.
Arguments:
- adjoint_state: float32 [4, 4, 64, 8192], P('inst', None, None, ('sector', 'slab')), may hold values from -6 to 6
- mean_flow: float32 [3, 8192], P(None, ('sector', 'slab')), may hold values from -0.5 to 0.5
- metric: float32 [3, 8192], P(None, ('sector', 'slab')), may hold values from 0.5 to 2
- connectivity: int32 [6, 8192], P(None, ('sector', 'slab')), may hold values from 0 to 1279, as said below
- wall_flags: int32 [6, 8192], P(None, ('sector', 'slab')), may hold values 0 or 1
- donor_face_positions: int32 [4, 2048], P('inst', ('sector', 'slab')), may hold values from 0 to 510, as said below
- interp_weight: float32 [4], P('inst'), may hold values from 0 to 1
Outputs:
- residual: float32 [4, 4, 64, 8192], P('inst', None, None, ('sector', 'slab'))
- new_state: float32 [4, 4, 64, 8192], P('inst', None, None, ('sector', 'slab'))
The draws below stay inside these ranges and needn't reach their ends.
Inputs may be any that keep to these rules, and one draw needn't show every extreme that they name: `connectivity`: within each block of 1024 columns: faces 0 to 3, face 4 of elements 256 and above and face 5 of elements below 768 name a local element below 1024; face 4 of the first 256 elements and face 5 of the last 256 elements name 1024 plus a distinct row of the neighbouring slab's layer. `donor_face_positions`: in each block of 256 columns, entry i of row t is i plus a rotation of instance t that is the same in every block.
All inputs are finite; a program needn't handle non-finite values. No bound on the sum of `wall_flags` on one device may be relied on, other than what follows from the above.
Results may differ from the reference program's by a relative error of at most 0.0003.
Values sent between devices are 32-bit elements; how exact they have to be, the bound alone decides.
No kernel may reach another device: no remote copies, remote signals or barrier semaphores. Data moves between devices by JAX's collectives and lax.ppermute only.
A program may use at most 192 MiB of HBM per device.

```python
import math
import jax
import jax.numpy as jnp
import numpy as np
from jax import lax

VARS = 4
NODES = 64
E_DEV = 1024
R_SLAB = 256
F_IF = 256
NT = 4
ELEMS = 8192
FACES_IF = 2048
N_INST = 4
N_SECTOR = 4
N_SLAB = 2


def permute_rows(key):
    return jax.random.permutation(key, R_SLAB).astype(jnp.int32)


def draw_connectivity(key, part):
    block_list = ELEMS // E_DEV
    subkeys = jax.random.split(key, 3)
    inner = jax.random.randint(subkeys[0], (6, block_list, E_DEV), 0, E_DEV).astype(jnp.int32)
    low_perm = jax.vmap(permute_rows)(jax.random.split(subkeys[1], block_list))
    high_perm = jax.vmap(permute_rows)(jax.random.split(subkeys[2], block_list))
    position = jnp.arange(E_DEV, dtype=jnp.int32)[None, :]
    pad_low = jnp.pad(low_perm, ((0, 0), (0, E_DEV - R_SLAB)))
    pad_high = jnp.pad(high_perm, ((0, 0), (E_DEV - R_SLAB, 0)))
    row_four = jnp.where(position < R_SLAB, E_DEV + pad_low, inner[4])
    row_five = jnp.where(position >= E_DEV - R_SLAB, E_DEV + pad_high, inner[5])
    joined = jnp.concatenate([inner[:4], row_four[None], row_five[None]], axis=0)
    return joined.reshape(6, ELEMS).astype(jnp.int32)


def draw_donor_face_positions(key, part):
    subkeys = jax.random.split(key, 3)
    rotation = jax.random.randint(subkeys[0], (NT,), 0, F_IF).astype(jnp.int32)
    widest = jax.random.randint(subkeys[1], (), 0, NT)
    other_one = (widest + 1 + jax.random.randint(subkeys[2], (), 0, NT - 1)) % NT
    rotation = rotation.at[widest].set(F_IF - 1).at[other_one].set(0)
    face_pos = jnp.arange(F_IF, dtype=jnp.int32)
    donor_table = rotation[:, None, None] + face_pos[None, None, :]
    return jnp.broadcast_to(donor_table, (NT, FACES_IF // F_IF, F_IF)).reshape(NT, FACES_IF).astype(jnp.int32)


def place_ends(values, rng, least, largest):
    shape = values.shape
    spot = [jax.random.randint(jax.random.fold_in(rng, axis), (), 0, shape[axis]) for axis in range(len(shape))]
    values = values.at[tuple(spot)].set(least)
    longest = shape.index(max(shape))
    spot[longest] = (spot[longest] + 1) % shape[longest]
    return values.at[tuple(spot)].set(largest)


def steps_of(key, shape, cuts, smallest, largest):
    gain = 1.0
    for dim, shards_of in cuts:
        draws = jax.random.uniform(jax.random.fold_in(jax.random.fold_in(key, 6), dim), (shards_of,), jnp.float32, smallest / len(cuts), largest / len(cuts))
        gain = gain * jnp.repeat(jnp.exp(draws), shape[dim] // shards_of).reshape((-1,) + (1,) * (len(shape) - 1 - dim))
    return gain


def noise(key, extent, deviation, limit, shards=(), kind=jnp.bfloat16):
    factor_of = steps_of(key, extent, shards, -0.22, 0.18) if shards else 1.0
    entries = jax.random.normal(key, extent, jnp.float32) * deviation * factor_of
    return jnp.minimum(jnp.maximum(entries, -limit), limit).astype(kind)


def setup_inputs(seed: int = 0) -> dict:
    arg_keys = jax.random.split(jax.random.key(seed), 8)
    adjoint_state = noise(arg_keys[0], (NT, VARS, NODES, ELEMS), 1.0, 6.0, ((0, 4), (3, 8)), jnp.float32)
    mean_flow = jnp.clip(jax.random.uniform(arg_keys[1], (3, ELEMS), jnp.float32, -0.5, 0.5) * steps_of(arg_keys[1], (3, ELEMS), ((1, 8),), -0.4, 0.0), -0.5, 0.5)
    metric = jnp.clip(jnp.exp(math.log(2.0) - 1.3862944 * jax.random.uniform(arg_keys[2], (3, ELEMS), jnp.float32) ** steps_of(arg_keys[2], (3, ELEMS), ((1, 8),), -0.2, 0.2)), 0.5, 2.0)
    connectivity = draw_connectivity(jax.random.fold_in(arg_keys[7], 71), 0)
    wall_flags = place_ends((jax.random.randint(arg_keys[4], (6, ELEMS), 0, 8) < 1).astype(jnp.int32), jax.random.fold_in(arg_keys[4], 1), 0, 1)
    donor_face_positions = draw_donor_face_positions(jax.random.fold_in(arg_keys[7], 71), 0)
    interp_weight = jnp.clip(1.0 * jax.random.uniform(arg_keys[6], (NT,), jnp.float32) ** steps_of(arg_keys[6], (NT,), ((0, 4),), -0.2, 0.2), 0.0, 1.0)
    return {"adjoint_state": adjoint_state, "mean_flow": mean_flow, "metric": metric, "connectivity": connectivity, "wall_flags": wall_flags, "donor_face_positions": donor_face_positions, "interp_weight": interp_weight}


omega_scale = 0.5
nyquist_damping = 0.5
wave_bound = 1.5
pseudo_step = 0.05
maximum_harmonic = lax.Precision.HIGHEST

def derivative_tables():
    points = np.array([-1.0, -1.0 / math.sqrt(5.0), 1.0 / math.sqrt(5.0), 1.0])
    weights = np.array([1.0 / np.prod([points[i] - points[m] for m in range(4) if m != i]) for i in range(4)])
    matrix = np.zeros((4, 4))
    for i in range(4):
        for j in range(4):
            if i != j:
                matrix[i, j] = weights[j] / weights[i] / (points[i] - points[j])
        matrix[i, i] = -np.sum(matrix[i])
    identity = np.eye(4)
    return np.stack([np.kron(np.kron(matrix, identity), identity), np.kron(np.kron(identity, matrix), identity), np.kron(np.kron(identity, identity), matrix)])

def spectral_matrix(count):
    row_index = jnp.arange(count, dtype=jnp.int32)[:, None]
    col_index = jnp.arange(count, dtype=jnp.int32)[None, :]
    offset = row_index - col_index
    parity = (1 - 2 * (offset % 2)).astype(jnp.float32)
    phase_angle = math.pi / count * offset.astype(jnp.float32)
    off_diag = offset != 0
    sine_val = jnp.where(off_diag, jnp.sin(phase_angle), 1.0)
    time_deriv = jnp.where(off_diag, 0.5 * parity * jnp.cos(phase_angle) / sine_val, 0.0)
    return -omega_scale * time_deriv - nyquist_damping / count * parity

def face_traces(block_adjoint_state):
    variables = block_adjoint_state.shape[0]
    elements = block_adjoint_state.shape[2]
    node_cube = block_adjoint_state.reshape(variables, 4, 4, 4, elements)
    traces = []
    for f in range(6):
        layer_pos = 0 if f % 2 == 0 else 3
        face_nodes = lax.index_in_dim(node_cube, layer_pos, 1 + f // 2, keepdims=False)
        traces.append(face_nodes.reshape(variables, 16, elements))
    return traces

def block_residual(block_adjoint_state, spectral_term, differentiation_tables, traces, mean_flow, metric, connectivity, wall_flags, ghost_low, ghost_high, iface_next, donor_face_positions, interp_weight):
    variables = block_adjoint_state.shape[0]
    elements = block_adjoint_state.shape[2]
    iface_count = iface_next.shape[2]
    pseudo_gradient = jnp.einsum('fga,cat->fcgt', differentiation_tables, block_adjoint_state, precision=maximum_harmonic) * metric[:, None, None, :]
    advection = lax.optimization_barrier(jnp.sum(mean_flow[:, None, None, :] * pseudo_gradient, axis=0))
    coupling = jnp.stack([pseudo_gradient[0, 1] + pseudo_gradient[1, 2] + pseudo_gradient[2, 3], pseudo_gradient[0, 0], pseudo_gradient[1, 0], pseudo_gradient[2, 0]])
    residual = advection + coupling + spectral_term
    residual_cube = residual.reshape(variables, 4, 4, 4, elements)
    tables = [traces[0], traces[1], traces[2], traces[3], jnp.concatenate([traces[4], ghost_high], axis=2), jnp.concatenate([traces[5], ghost_low], axis=2)]
    for f in range(6):
        k = f // 2
        orient = -1.0 if f % 2 == 0 else 1.0
        own_trace = traces[f]
        neighbour = jnp.take(tables[f ^ 1], connectivity[f], axis=2)
        mirror_sign = jnp.ones((variables,), jnp.float32).at[1 + k].set(-1.0)
        mirrored = own_trace * mirror_sign[:, None, None]
        neighbour = jnp.where(wall_flags[f][None, None, :] == 1, mirrored, neighbour)
        if f == 1:
            interface_rows = jnp.concatenate([own_trace[:, :, elements - iface_count:], iface_next], axis=2)
            lower_val = jnp.take(interface_rows, donor_face_positions, axis=2)
            upper_val = jnp.take(interface_rows, donor_face_positions + 1, axis=2)
            blended = (1.0 - interp_weight) * lower_val + interp_weight * upper_val
            neighbour = jnp.concatenate([neighbour[:, :, :elements - iface_count], blended], axis=2)
        face_jump = neighbour - own_trace
        flux_jump = orient * mean_flow[k][None, None, :] * face_jump
        zero_row = jnp.zeros_like(face_jump[0])
        cross_terms = []
        for v in range(4):
            if v == 0:
                cross_terms.append(orient * face_jump[1 + k])
            elif v == 1 + k:
                cross_terms.append(orient * face_jump[0])
            else:
                cross_terms.append(zero_row)
        flux_jump = flux_jump + jnp.stack(cross_terms)
        lifted = 3.0 * metric[k][None, None, :] * (flux_jump + wave_bound * face_jump)
        layer_pos = 0 if f % 2 == 0 else 3
        face_slot = (slice(None),) * (1 + k) + (layer_pos,)
        residual_cube = residual_cube.at[face_slot].add(lifted.reshape(variables, 4, 4, elements))
    return residual_cube.reshape(variables, 64, elements)

def reference(adjoint_state, mean_flow, metric, connectivity, wall_flags, donor_face_positions, interp_weight):
    block_list = N_SECTOR * N_SLAB
    differentiation_tables = jnp.asarray(derivative_tables(), jnp.float32)
    spectral = spectral_matrix(N_INST)
    flat_state = adjoint_state.reshape(N_INST, -1)
    spectral_operator_full = jnp.dot(spectral, flat_state, precision=maximum_harmonic, preferred_element_type=jnp.float32).reshape(N_INST, VARS, NODES, block_list, E_DEV)
    state_blocks = adjoint_state.reshape(N_INST, VARS, NODES, block_list, E_DEV)
    flow_blocks = jnp.moveaxis(mean_flow.reshape(3, block_list, E_DEV), 1, 0)
    metric_blocks = jnp.moveaxis(metric.reshape(3, block_list, E_DEV), 1, 0)
    conn_blocks = jnp.moveaxis(connectivity.reshape(6, block_list, E_DEV), 1, 0)
    flag_blocks = jnp.moveaxis(wall_flags.reshape(6, block_list, E_DEV), 1, 0)
    donor_blocks = donor_face_positions.reshape(N_INST, block_list, F_IF)

    def one_instance(packed):
        state_inst, spectral_inst, donor_inst, weight_inst = packed
        per_block = jnp.moveaxis(state_inst, 2, 0)
        spectral_block = jnp.moveaxis(spectral_inst, 2, 0)
        traces = jax.vmap(face_traces)(per_block)
        top_layer = traces[5][..., E_DEV - R_SLAB:].reshape(N_SECTOR, N_SLAB, VARS, 16, R_SLAB)
        bottom_layer = traces[4][..., :R_SLAB].reshape(N_SECTOR, N_SLAB, VARS, 16, R_SLAB)
        empty_layer = jnp.zeros_like(top_layer[:, :1])
        ghost_low = jnp.concatenate([empty_layer, top_layer[:, :-1]], axis=1).reshape(block_list, VARS, 16, R_SLAB)
        ghost_high = jnp.concatenate([bottom_layer[:, 1:], empty_layer], axis=1).reshape(block_list, VARS, 16, R_SLAB)
        own_iface = traces[1][..., E_DEV - F_IF:].reshape(N_SECTOR, N_SLAB, VARS, 16, F_IF)
        iface_next = jnp.roll(own_iface, -1, axis=0).reshape(block_list, VARS, 16, F_IF)
        result = jax.vmap(block_residual, in_axes=(0, 0, None, 0, 0, 0, 0, 0, 0, 0, 0, 0, None))(per_block, spectral_block, differentiation_tables, traces, flow_blocks, metric_blocks, conn_blocks, flag_blocks, ghost_low, ghost_high, iface_next, donor_inst, weight_inst)
        return jnp.moveaxis(result, 0, 2)
    residual = lax.map(one_instance, (state_blocks, spectral_operator_full, donor_blocks, interp_weight))
    residual = residual.reshape(N_INST, VARS, NODES, block_list * E_DEV)
    return (residual, adjoint_state + pseudo_step * residual)
```

```python
import math

import jax
import jax.numpy as jnp
import numpy as np
from jax import lax
from jax.sharding import PartitionSpec as P

omega_scale = 0.5
nyquist_damping = 0.5
wave_bound = 1.5
pseudo_step = 0.05
maximum_harmonic = lax.Precision.HIGHEST


def padded_2(value, sides, width):
    for axis, dim in sides:
        size, length = (lax.axis_size(axis), value.shape[dim])
        up = [(i, (i + 1) % size) for i in range(size - 1)]
        down = [(j, i) for i, j in up]
        last = lax.slice_in_dim(value, length - width, length, axis=dim)
        leading = lax.slice_in_dim(value, 0, width, axis=dim)
        before = lax.ppermute(last, axis, up)
        after = lax.ppermute(leading, axis, down)
        value = jnp.concatenate([before, value, after], axis=dim)
    return value


def passed_along(value, axis, by):
    length = lax.axis_size(axis)
    return lax.ppermute(value, axis, [(i, (i + by) % length) for i in range(length)])


def derivative_tables():
    points = np.array([-1.0, -1.0 / math.sqrt(5.0), 1.0 / math.sqrt(5.0), 1.0])
    weights = np.array(
        [1.0 / np.prod([points[i] - points[m] for m in range(4) if m != i]) for i in range(4)]
    )
    matrix = np.zeros((4, 4))
    for i in range(4):
        for j in range(4):
            if i != j:
                matrix[i, j] = weights[j] / weights[i] / (points[i] - points[j])
        matrix[i, i] = -np.sum(matrix[i])
    identity = np.eye(4)
    return np.stack(
        [
            np.kron(np.kron(matrix, identity), identity),
            np.kron(np.kron(identity, matrix), identity),
            np.kron(np.kron(identity, identity), matrix),
        ]
    )


def selection_table():
    selector_matrix = np.zeros((96, 64))
    for f in range(6):
        k = f // 2
        layer_pos = 0 if f % 2 == 0 else 3
        for first in range(4):
            for second in range(4):
                indices = [first, second]
                indices.insert(k, layer_pos)
                selector_matrix[
                    16 * f + 4 * first + second, 16 * indices[0] + 4 * indices[1] + indices[2]
                ] = 1.0
    return selector_matrix


def spectral_matrix(count):
    offset = np.arange(count)[:, None] - np.arange(count)[None, :]
    parity = 1.0 - 2.0 * (offset % 2)
    angle = np.pi * offset / count
    off_diag = offset != 0
    sine = np.where(off_diag, np.sin(angle), 1.0)
    time_deriv = np.where(off_diag, 0.5 * parity * np.cos(angle) / sine, 0.0)
    return -omega_scale * time_deriv - nyquist_damping / count * parity


def group_split(count):
    outer = max(d for d in range(1, count + 1) if count % d == 0 and d * d <= count)
    return outer, count // outer


def spectral_pieces(pieces, axis):
    count = lax.axis_size(axis)
    outer, inner = group_split(count)
    place = lambda p, q: (p % outer) * inner + q % inner
    weights = np.zeros((count, inner, outer))
    matrix = spectral_matrix(count)
    for p in range(outer):
        for q in range(inner):
            for t in range(inner):
                for r in range(outer):
                    weights[place(p, q), t, r] = matrix[place(p, q + t), place(p - r, q)]
    mine = lax.dynamic_index_in_dim(
        jnp.asarray(weights, jnp.float32), lax.axis_index(axis), 0, keepdims=False
    )
    spots = [(p, q) for p in range(outer) for q in range(inner)]
    gathered = []
    for piece in pieces:
        held = [piece]
        for r in range(1, outer):
            pairs = [(place(p, q), place(p + r, q)) for p, q in spots]
            held.append(lax.ppermute(piece, axis, pairs))
        gathered.append(held)
    sums = []
    for held in gathered:
        total = sum(mine[0, r] * held[r] for r in range(outer))
        for t in range(1, inner):
            pairs = [(place(p, q), place(p, q + t)) for p, q in spots]
            send = sum(mine[t, r] * held[r] for r in range(outer))
            total = total + lax.ppermute(send, axis, pairs)
        sums.append(total)
    return sums


def lookup_columns(lookup_table, columns):
    length = lookup_table.shape[2]
    indicator_matrix = (jnp.arange(length, dtype=jnp.int32)[:, None] == columns[None, :]).astype(
        jnp.float32
    )
    return jnp.einsum("xiz,zy->xiy", lookup_table, indicator_matrix, precision=maximum_harmonic)


def body_residual(
    state_of_block,
    spectral_term,
    differentiation_tables,
    selector_matrix,
    traces,
    mean_flow,
    metric,
    connectivity,
    wall_flags,
    ghost_low,
    ghost_high,
    iface_next,
    donor_positions,
    weight_value,
):
    variables = state_of_block.shape[0]
    elements = state_of_block.shape[2]
    iface_count = iface_next.shape[2]
    pseudo_gradient = (
        jnp.einsum(
            "fga,cat->fcgt", differentiation_tables, state_of_block, precision=maximum_harmonic
        )
        * metric[:, None, None, :]
    )
    advection = jnp.sum(mean_flow[:, None, None, :] * pseudo_gradient, axis=0)
    coupling = jnp.stack(
        [
            pseudo_gradient[0, 1] + pseudo_gradient[1, 2] + pseudo_gradient[2, 3],
            pseudo_gradient[0, 0],
            pseudo_gradient[1, 0],
            pseudo_gradient[2, 0],
        ]
    )
    residual = advection + coupling + spectral_term
    tables = [
        traces[0],
        traces[1],
        traces[2],
        traces[3],
        jnp.concatenate([traces[4], ghost_high], axis=2),
        jnp.concatenate([traces[5], ghost_low], axis=2),
    ]
    lifted_faces = []
    for f in range(6):
        k = f // 2
        orient = -1.0 if f % 2 == 0 else 1.0
        own_trace = traces[f]
        neighbour = lookup_columns(tables[f ^ 1], connectivity[f])
        mirror_sign = jnp.ones((variables,), jnp.float32).at[1 + k].set(-1.0)
        mirrored = own_trace * mirror_sign[:, None, None]
        neighbour = jnp.where(wall_flags[f][None, None, :] == 1, mirrored, neighbour)
        if f == 1:
            interface_rows = jnp.concatenate(
                [own_trace[:, :, elements - iface_count :], iface_next], axis=2
            )
            row_ids = jnp.arange(2 * iface_count, dtype=jnp.int32)[:, None]
            mixing_weight_matrix = (1.0 - weight_value) * (
                row_ids == donor_positions[None, :]
            ).astype(jnp.float32) + weight_value * (row_ids == donor_positions[None, :] + 1).astype(
                jnp.float32
            )
            blended = jnp.einsum(
                "xiz,zy->xiy", interface_rows, mixing_weight_matrix, precision=maximum_harmonic
            )
            neighbour = jnp.concatenate(
                [neighbour[:, :, : elements - iface_count], blended], axis=2
            )
        face_jump = neighbour - own_trace
        flux_jump = orient * mean_flow[k][None, None, :] * face_jump
        zero_row = jnp.zeros_like(face_jump[0])
        cross_terms = []
        for v in range(4):
            if v == 0:
                cross_terms.append(orient * face_jump[1 + k])
            elif v == 1 + k:
                cross_terms.append(orient * face_jump[0])
            else:
                cross_terms.append(zero_row)
        flux_jump = flux_jump + jnp.stack(cross_terms)
        lifted_faces.append(3.0 * metric[k][None, None, :] * (flux_jump + wave_bound * face_jump))
    lifted_everything = jnp.concatenate(lifted_faces, axis=1)
    return residual + jnp.einsum(
        "bc,sbh->sch", selector_matrix, lifted_everything, precision=maximum_harmonic
    )


def per_device(
    adjoint_state, mean_flow, metric, connectivity, wall_flags, donor_face_positions, interp_weight
):
    state_of_block = adjoint_state[0]
    variables, node_count, elements = state_of_block.shape
    rim_width = elements // 4
    iface_count = donor_face_positions.shape[1]
    differentiation_tables = jnp.asarray(derivative_tables(), jnp.float32)
    selector_matrix = jnp.asarray(selection_table(), jnp.float32)
    every_trace_set = jnp.einsum(
        "qa,yas->yqs", selector_matrix, state_of_block, precision=maximum_harmonic
    )
    traces = [every_trace_set[:, 16 * f : 16 * f + 16, :] for f in range(6)]
    slab_edge_rows = jnp.concatenate(
        [traces[4][:, :, :rim_width], traces[5][:, :, elements - rim_width :]], axis=2
    )
    padded = padded_2(slab_edge_rows, (("slab", 2),), rim_width)
    ghost_low = padded[:, :, :rim_width]
    ghost_high = padded[:, :, 3 * rim_width :]
    iface_next = passed_along(traces[1][:, :, elements - iface_count :], "sector", -1)
    spectral_term = jnp.concatenate(
        spectral_pieces([state_of_block[v : v + 1] for v in range(variables)], "inst"), axis=0
    )
    residual = body_residual(
        state_of_block,
        spectral_term,
        differentiation_tables,
        selector_matrix,
        traces,
        mean_flow,
        metric,
        connectivity,
        wall_flags,
        ghost_low,
        ghost_high,
        iface_next,
        donor_face_positions[0],
        interp_weight[0],
    )
    return (residual[None], (state_of_block + pseudo_step * residual)[None])


def solution(mesh):
    return jax.shard_map(
        per_device,
        mesh=mesh,
        in_specs=(
            P("inst", None, None, ("sector", "slab")),
            P(None, ("sector", "slab")),
            P(None, ("sector", "slab")),
            P(None, ("sector", "slab")),
            P(None, ("sector", "slab")),
            P("inst", ("sector", "slab")),
            P("inst"),
        ),
        out_specs=(
            P("inst", None, None, ("sector", "slab")),
            P("inst", None, None, ("sector", "slab")),
        ),
        check_vma=False,
    )
```
